32 devices in a mesh: pipe: 2 (over x), ep: 16 (over z, y, core).
Axes of the slice: x: 2, y: 2, z: 4, core: 2. Of those that a mesh axis runs over, the one named last changes fastest.
Arguments:
- fresh: bfloat16 [2, 1024, 3584], P(None, 'ep'), may hold values from -48 to 48
- pending: bfloat16 [1024, 3584], P('ep'), may hold values from -48 to 48
- expert_ids: int32 [2, 2, 1024, 8], P('pipe', None, 'ep'), may hold values from 0 to 15, as said below
- chosen_groups: int32 [2, 2, 1024, 4], P('pipe', None, 'ep'), may hold values from 0 to 7, as said below
- affinity: float32 [2, 2, 1024, 8], P('pipe', None, 'ep'), may hold values from 0.05 to 1
- norm_gain: float32 [2, 3584], P('pipe'), may hold values from 0.25 to 1.75
- w_gate_up: bfloat16 [2, 16, 3584, 2048], P('pipe', 'ep'), may hold values from -0.09375 to 0.09375
- w_down: bfloat16 [2, 16, 1024, 3584], P('pipe', 'ep'), may hold values from -0.1875 to 0.1875
Outputs:
- section_out: bfloat16 [2, 2, 1024, 3584], P('pipe', None, 'ep')
The draws below stay inside these ranges and needn't reach their ends.
Inputs may be any that keep to these rules, and one draw needn't show every extreme that they name: `expert_ids`: each row names 8 different experts. Within one section and slot, the rows of one device (aligned blocks of 64 rows) name one expert at most 63 times, and in every such block some expert is named exactly 63 times. `chosen_groups`: each row names 4 different groups; expert e lies in group e // 2. A row's experts may lie outside its groups.
All inputs are finite; a program needn't handle non-finite values.
Results may differ from the reference program's by a relative error of at most 0.0052.
Values may be sent and summed in bfloat16 or wider, within the bound.
A program may use at most 128 MiB of HBM per device.

```python
import math
import jax
import jax.numpy as jnp
from jax import lax

D = 3584
FF = 1024
TOP = 8
GROUPS = 8
GSEL = 4
MICRO = 2
TOK_MB = 64
EXPERTS = 16
TOKENS = 1024
CAP = 63
N_EP = 16


def route_tables(key):
    base_key = jax.random.fold_in(key, 7)
    device_count = TOKENS // TOK_MB
    block_count = 2 * MICRO * device_count
    per_group = EXPERTS // GROUPS
    expert_iota = jnp.arange(EXPERTS, dtype=jnp.int32)
    group_iota = jnp.arange(GROUPS, dtype=jnp.int32)
    pick_key, popular_key, blocks_key = jax.random.split(base_key, 3)
    favored = jax.random.randint(pick_key, (2 * MICRO,), 0, EXPERTS)
    popular = jax.random.randint(popular_key, (2 * MICRO, EXPERTS), 0, 4)
    block_keys = jax.random.split(blocks_key, block_count)
    block_owner = jnp.arange(block_count, dtype=jnp.int32) // device_count

    def one_block(block_key, favorite, popularity):
        group_key, score_key, intruder_key, flag_key = jax.random.split(block_key, 4)
        group_score = jax.random.randint(group_key, (TOK_MB, GROUPS), 0, 1024) * GROUPS + group_iota
        forced = (jnp.arange(TOK_MB) < CAP)[:, None] & (group_iota == favorite // per_group)[None, :]
        group_score = group_score + forced.astype(jnp.int32) * (2048 * GROUPS)
        _, selected = lax.top_k(group_score, GSEL)
        member = jnp.any((expert_iota // per_group)[None, :, None] == selected[:, None, :], axis=-1)
        intruder_score = jax.random.randint(intruder_key, (TOK_MB, EXPERTS), 0, 1024) * EXPERTS + expert_iota
        intruder_score = jnp.where(member, -1, intruder_score)
        _, intruder = lax.top_k(intruder_score, 1)
        flagged = jax.random.randint(flag_key, (TOK_MB,), 0, 4) == 0
        extra_pick = (expert_iota[None, :] == intruder) & flagged[:, None]
        jitter = jax.random.randint(score_key, (TOK_MB, EXPERTS), 0, 256) * EXPERTS + expert_iota
        tier_level = jnp.where(member | extra_pick, 3, 1) + jnp.where(member & (expert_iota == favorite)[None, :], 1, 0)
        ranked = tier_level * (1024 * EXPERTS) + popularity[None, :] * (256 * EXPERTS) + jitter

        def step_token(counts, rank_row):
            usable = counts < CAP
            masked_score = jnp.where(usable, rank_row, -1 - expert_iota)
            _, chosen = lax.top_k(masked_score, TOP)
            counts = counts + jnp.sum((chosen[:, None] == expert_iota[None, :]).astype(jnp.int32), axis=0)
            return (counts, chosen)
        _, chosen = lax.scan(step_token, jnp.zeros((EXPERTS,), jnp.int32), ranked)
        return (chosen, selected)
    chosen, selected = jax.vmap(one_block)(block_keys, favored[block_owner], popular[block_owner])
    return (chosen.reshape(2, MICRO, TOKENS, TOP).astype(jnp.int32), selected.reshape(2, MICRO, TOKENS, GSEL).astype(jnp.int32))


def draw_expert_ids(key, part):
    return route_tables(key)[0]


def draw_chosen_groups(key, part):
    return route_tables(key)[1]


def scaled_rows(key, row_count):
    base_key, row_key, column_key = jax.random.split(key, 3)
    values = jnp.clip(jax.random.normal(base_key, (row_count, D), jnp.float32), -4.0, 4.0)
    column_scale = jnp.exp(jax.random.uniform(column_key, (1, D), jnp.float32, math.log(0.4), math.log(4.0)))
    row_scale = jnp.exp(jax.random.uniform(row_key, (row_count, 1), jnp.float32, math.log(0.3), math.log(3.0)))
    return values * row_scale * column_scale


def draw_fresh(key, part):
    values = scaled_rows(jax.random.fold_in(key, 11), MICRO * TOKENS)
    return values.reshape(MICRO, TOKENS, D).astype(jnp.bfloat16)


def draw_pending(key, part):
    return scaled_rows(jax.random.fold_in(key, 13), TOKENS).astype(jnp.bfloat16)


def steps_of(stream_key, dims, shards, smallest, largest):
    factor_of, own = 1.0, jax.random.fold_in(stream_key, 6)
    for dim, blocks in shards:
        heights = jnp.exp(jax.random.uniform(jax.random.fold_in(own, dim), (blocks,), jnp.float32, smallest / len(shards), largest / len(shards)))
        factor_of = factor_of * jnp.repeat(heights, dims[dim] // blocks).reshape([-1 if axis == dim else 1 for axis in range(len(dims))])
    return factor_of


def centred(stream_key, shape, width, reach, shards=(), kind=jnp.bfloat16):
    array = jax.random.normal(stream_key, shape, jnp.float32) * width
    if len(shards) > 0:
        array = steps_of(stream_key, shape, shards, -0.22, 0.18) * array
    return jnp.clip(array, min=-reach, max=reach).astype(kind)


def setup_inputs(seed: int = 0) -> dict:
    arg_keys = jax.random.split(jax.random.key(seed), 9)
    fresh = draw_fresh(jax.random.fold_in(arg_keys[8], 71), 0)
    pending = draw_pending(jax.random.fold_in(arg_keys[8], 71), 0)
    expert_ids = draw_expert_ids(jax.random.fold_in(arg_keys[8], 71), 0)
    chosen_groups = draw_chosen_groups(jax.random.fold_in(arg_keys[8], 71), 0)
    affinity = jnp.clip(jnp.exp(math.log(1.0) - 2.9957323 * jax.random.uniform(arg_keys[4], (2, MICRO, TOKENS, TOP), jnp.float32) ** steps_of(arg_keys[4], (2, MICRO, TOKENS, TOP), ((0, 2), (2, 16)), -0.2, 0.2)), 0.05, 1.0)
    norm_gain = jnp.clip(1.0 + 0.15 * jax.random.normal(arg_keys[5], (2, D), jnp.float32), 0.25, 1.75)
    w_gate_up = centred(arg_keys[6], (2, EXPERTS, D, 2 * FF), D ** -0.5, 0.09375, ((0, 2), (1, 16)))
    w_down = centred(arg_keys[7], (2, EXPERTS, FF, D), FF ** -0.5, 0.1875, ((0, 2), (1, 16)))
    return dict(fresh=fresh, pending=pending, expert_ids=expert_ids, chosen_groups=chosen_groups, affinity=affinity, norm_gain=norm_gain, w_gate_up=w_gate_up, w_down=w_down)


EPSILON = 1e-06
ROUTED_SCALE = 2.5

def rms_scale(hidden, gain):
    widened = hidden.astype(jnp.float32)
    mean_square = lax.optimization_barrier(jnp.mean(widened * widened, axis=-1, keepdims=True))
    return (widened * lax.rsqrt(mean_square + EPSILON) * gain.astype(jnp.float32)).astype(jnp.bfloat16)

def gate_table(routes, groups, affinity):
    per_group = EXPERTS // GROUPS
    owners = routes // per_group
    in_group = jnp.any(owners[:, :, None] == groups[:, None, :], axis=-1)
    summed = lax.optimization_barrier(jnp.sum(affinity, axis=-1, keepdims=True))
    return ROUTED_SCALE * affinity * in_group.astype(jnp.float32) / summed

def slot_table(routes):
    blocks = routes.reshape(N_EP, TOK_MB, TOP)
    matches = (blocks[..., None] == jnp.arange(EXPERTS, dtype=jnp.int32)).astype(jnp.int32)
    per_token = lax.optimization_barrier(jnp.sum(matches, axis=2))
    earlier = jnp.cumsum(per_token, axis=1) - per_token
    return lax.optimization_barrier(jnp.sum(matches * earlier[:, :, None, :], axis=-1)).astype(jnp.int32)

def expert_layer(hidden, routes, groups, affinity, gain, w_gate_up, w_down):
    normed = rms_scale(hidden, gain)
    weights = gate_table(routes, groups, affinity).reshape(N_EP, TOK_MB, TOP)
    position = slot_table(routes)
    blocks = routes.reshape(N_EP, TOK_MB, TOP)
    normed_blocks = normed.reshape(N_EP, TOK_MB, D).astype(jnp.float32)
    slot_iota = jnp.arange(CAP, dtype=jnp.int32)

    def one_expert(running, packed):
        expert_index, gate_up, down_proj = packed
        chosen = blocks == expert_index
        slot_hit = chosen[..., None] & (position[..., None] == slot_iota)
        occupied = jnp.any(slot_hit, axis=2).astype(jnp.float32)
        slot_rows = jnp.einsum('btc,btd->bcd', occupied, normed_blocks)
        slot_rows = slot_rows.reshape(N_EP * CAP, D).astype(jnp.bfloat16)
        joined = jnp.dot(slot_rows, gate_up, preferred_element_type=jnp.float32)
        active = (jax.nn.silu(joined[:, :FF]) * joined[:, FF:]).astype(jnp.bfloat16)
        produced = jnp.dot(active, down_proj, preferred_element_type=jnp.float32).astype(jnp.bfloat16)
        produced = produced.reshape(N_EP, CAP, D).astype(jnp.float32)
        scaling = lax.optimization_barrier(jnp.sum(jnp.where(slot_hit, weights[..., None], jnp.float32(0.0)), axis=2))
        added = jnp.einsum('btc,bcd->btd', scaling, produced)
        return (running + added.reshape(TOKENS, D), None)
    start = jnp.zeros((TOKENS, D), jnp.float32)
    running, _ = lax.scan(one_expert, start, (jnp.arange(EXPERTS, dtype=jnp.int32), w_gate_up, w_down))
    return (hidden.astype(jnp.float32) + running).astype(jnp.bfloat16)

def reference(fresh, pending, expert_ids, chosen_groups, affinity, norm_gain, w_gate_up, w_down):

    def run_slot(section_index, slot_index, layer_in):
        return expert_layer(layer_in, expert_ids[section_index, slot_index], chosen_groups[section_index, slot_index], affinity[section_index, slot_index], norm_gain[section_index], w_gate_up[section_index], w_down[section_index])
    first_out = run_slot(0, 0, fresh[0])
    second_out = run_slot(0, 1, fresh[1])
    third_out = run_slot(1, 0, pending)
    fourth_out = run_slot(1, 1, first_out)
    return jnp.stack([jnp.stack([first_out, second_out]), jnp.stack([third_out, fourth_out])])
```

```python
import jax
import jax.numpy as jnp
from jax import lax
from jax.sharding import PartitionSpec as P

TOP = 8
GROUPS = 8


EPSILON = 1e-06
ROUTED_SCALE = 2.5


def from_behind(value, axis, steps):
    count = lax.axis_size(axis)
    first, last = (max(0, -steps), min(count, count - steps))
    return lax.ppermute(value, axis, [(source, source + steps) for source in range(first, last)])


def rms_scale(hidden, gain):
    widened = hidden.astype(jnp.float32)
    mean_square = jnp.mean(widened * widened, axis=-1, keepdims=True)
    return (widened * lax.rsqrt(mean_square + EPSILON) * gain).astype(jnp.bfloat16)


def gate_table(routes, groups, affinity, experts):
    per_group = experts // GROUPS
    owners = routes // per_group
    in_group = jnp.any(owners[:, :, None] == groups[:, None, :], axis=-1)
    summed = jnp.sum(affinity, axis=-1, keepdims=True)
    return ROUTED_SCALE * affinity * in_group.astype(jnp.float32) / summed


def slot_capacity(tokens, experts):
    spread = tokens * TOP * 5 // (4 * experts)
    needed = ((tokens - 1) * TOP + experts - TOP - 1) // (experts - TOP)
    return min(tokens, max(spread, needed))


def moe_layer(hidden, routes, groups, affinity, gain, w_gate_up, w_down):
    experts = lax.axis_size("ep")
    tokens = hidden.shape[0]
    capacity = slot_capacity(tokens, experts)
    normed = rms_scale(hidden, gain)
    weights = gate_table(routes, groups, affinity, experts)
    expert_iota = jnp.arange(experts, dtype=jnp.int32)
    matches = (routes[:, :, None] == expert_iota).astype(jnp.int32)
    per_token = jnp.sum(matches, axis=1)
    earlier = jnp.cumsum(per_token, axis=0) - per_token
    position = jnp.sum(matches * earlier[:, None, :], axis=-1)
    slot_index = routes * capacity + position
    slot_iota = jnp.arange(experts * capacity, dtype=jnp.int32)
    placing = jnp.any(slot_iota[:, None, None] == slot_index[None, :, :], axis=-1).astype(
        jnp.bfloat16
    )
    outgoing = jnp.dot(placing, normed, preferred_element_type=jnp.float32).astype(jnp.bfloat16)
    outgoing = outgoing.reshape(experts, capacity, normed.shape[1])
    hidden_units = w_down.shape[2]
    arrived_rows = lax.all_to_all(outgoing, "ep", split_axis=0, concat_axis=0, tiled=True)
    flat_rows = arrived_rows.reshape(-1, arrived_rows.shape[-1])
    joined = jnp.dot(flat_rows, w_gate_up[0, 0], preferred_element_type=jnp.float32)
    active = (jax.nn.silu(joined[:, :hidden_units]) * joined[:, hidden_units:]).astype(jnp.bfloat16)
    produced = jnp.dot(active, w_down[0, 0], preferred_element_type=jnp.float32).astype(
        jnp.bfloat16
    )
    returned = lax.all_to_all(
        produced.reshape(arrived_rows.shape), "ep", split_axis=0, concat_axis=0, tiled=True
    )
    gathered = jnp.take(returned.reshape(experts * capacity, -1), slot_index, axis=0)
    layer_out = hidden.astype(jnp.float32) + jnp.sum(
        weights[:, :, None] * gathered.astype(jnp.float32), axis=1
    )
    return layer_out.astype(jnp.bfloat16)


def gathers_whole_blocks(tokens, experts):
    return 2 * slot_capacity(tokens, experts) > tokens


def gate_columns(routes, groups, affinity, experts):
    weights = gate_table(routes, groups, affinity, experts)
    expert_iota = jnp.arange(experts, dtype=jnp.int32)
    hit = routes[:, :, None] == expert_iota
    return jnp.sum(jnp.where(hit, weights[:, :, None], 0.0), axis=1)


def dense_layer(hidden, gates, gain, w_gate_up, w_down):
    normed = rms_scale(hidden, gain)
    hidden_units = w_down.shape[2]
    rows = lax.all_gather(normed, "ep", axis=0, tiled=True)
    joined = jnp.dot(rows, w_gate_up[0, 0], preferred_element_type=jnp.float32)
    active = (jax.nn.silu(joined[:, :hidden_units]) * joined[:, hidden_units:]).astype(jnp.bfloat16)
    produced = jnp.dot(active, w_down[0, 0], preferred_element_type=jnp.float32)
    scaled = (produced * gates[:, None]).astype(jnp.bfloat16)
    summed = lax.psum_scatter(scaled, "ep", scatter_dimension=0, tiled=True)
    return (hidden.astype(jnp.float32) + summed.astype(jnp.float32)).astype(jnp.bfloat16)


def per_device(fresh, pending, expert_ids, chosen_groups, affinity, norm_gain, w_gate_up, w_down):
    at_start = lax.axis_index("pipe") == 0

    tokens, experts = pending.shape[0], lax.axis_size("ep")
    gathering = gathers_whole_blocks(tokens, experts)
    if gathering:
        columns = jnp.stack(
            [
                gate_columns(expert_ids[0, j], chosen_groups[0, j], affinity[0, j], experts)
                for j in range(2)
            ]
        )
        columns = lax.all_to_all(columns, "ep", split_axis=2, concat_axis=1, tiled=True)[:, :, 0]

    def run_slot(place_index, layer_in):
        if gathering:
            return dense_layer(layer_in, columns[place_index], norm_gain[0], w_gate_up, w_down)
        return moe_layer(
            layer_in,
            expert_ids[0, place_index],
            chosen_groups[0, place_index],
            affinity[0, place_index],
            norm_gain[0],
            w_gate_up,
            w_down,
        )

    first_out = run_slot(0, jnp.where(at_start, fresh[0], pending))
    handed = from_behind(first_out, "pipe", 1)
    second_out = run_slot(1, jnp.where(at_start, fresh[1], handed))
    return jnp.stack([first_out, second_out])[None]


def solution(mesh):
    return jax.shard_map(
        per_device,
        mesh=mesh,
        in_specs=(
            P(None, "ep", None),
            P("ep", None),
            P("pipe", None, "ep", None),
            P("pipe", None, "ep", None),
            P("pipe", None, "ep", None),
            P("pipe", None),
            P("pipe", "ep", None, None),
            P("pipe", "ep", None, None),
        ),
        out_specs=P("pipe", None, "ep", None),
        check_vma=False,
    )
```

```python
import functools

import jax
import jax.numpy as jnp
from jax import lax
from jax.experimental import pallas as pl
from jax.experimental.pallas import tpu as pltpu
from jax.sharding import PartitionSpec as P

TOP = 8
GROUPS = 8


EPSILON = 1e-06
ROUTED_SCALE = 2.5


def from_behind(value, axis, steps):
    count = lax.axis_size(axis)
    first, last = (max(0, -steps), min(count, count - steps))
    return lax.ppermute(value, axis, [(source, source + steps) for source in range(first, last)])


def rms_scale(hidden, gain):
    widened = hidden.astype(jnp.float32)
    mean_square = jnp.mean(widened * widened, axis=-1, keepdims=True)
    return (widened * lax.rsqrt(mean_square + EPSILON) * gain).astype(jnp.bfloat16)


def gate_table(routes, groups, affinity, experts):
    per_group = experts // GROUPS
    owners = routes // per_group
    in_group = jnp.any(owners[:, :, None] == groups[:, None, :], axis=-1)
    summed = jnp.sum(affinity, axis=-1, keepdims=True)
    return ROUTED_SCALE * affinity * in_group.astype(jnp.float32) / summed


def slot_capacity(tokens, experts):
    spread = tokens * TOP * 5 // (4 * experts)
    needed = ((tokens - 1) * TOP + experts - TOP - 1) // (experts - TOP)
    return min(tokens, max(spread, needed))


def moe_layer(hidden, routes, groups, affinity, gain, w_gate_up, w_down):
    experts = lax.axis_size("ep")
    tokens = hidden.shape[0]
    capacity = slot_capacity(tokens, experts)
    normed = rms_scale(hidden, gain)
    weights = gate_table(routes, groups, affinity, experts)
    expert_iota = jnp.arange(experts, dtype=jnp.int32)
    matches = (routes[:, :, None] == expert_iota).astype(jnp.int32)
    per_token = jnp.sum(matches, axis=1)
    earlier = jnp.cumsum(per_token, axis=0) - per_token
    position = jnp.sum(matches * earlier[:, None, :], axis=-1)
    slot_index = routes * capacity + position
    slot_iota = jnp.arange(experts * capacity, dtype=jnp.int32)
    placing = jnp.any(slot_iota[:, None, None] == slot_index[None, :, :], axis=-1).astype(
        jnp.bfloat16
    )
    outgoing = jnp.dot(placing, normed, preferred_element_type=jnp.float32).astype(jnp.bfloat16)
    outgoing = outgoing.reshape(experts, capacity, normed.shape[1])
    hidden_units = w_down.shape[2]
    arrived_rows = lax.all_to_all(outgoing, "ep", split_axis=0, concat_axis=0, tiled=True)
    flat_rows = arrived_rows.reshape(-1, arrived_rows.shape[-1])
    joined = jnp.dot(flat_rows, w_gate_up[0, 0], preferred_element_type=jnp.float32)
    active = (jax.nn.silu(joined[:, :hidden_units]) * joined[:, hidden_units:]).astype(jnp.bfloat16)
    produced = jnp.dot(active, w_down[0, 0], preferred_element_type=jnp.float32).astype(
        jnp.bfloat16
    )
    returned = lax.all_to_all(
        produced.reshape(arrived_rows.shape), "ep", split_axis=0, concat_axis=0, tiled=True
    )
    gathered = jnp.take(returned.reshape(experts * capacity, -1), slot_index, axis=0)
    layer_out = hidden.astype(jnp.float32) + jnp.sum(
        weights[:, :, None] * gathered.astype(jnp.float32), axis=1
    )
    return layer_out.astype(jnp.bfloat16)


def gathers_whole_blocks(tokens, experts):
    return experts % 4 == 0 and experts > 4 and 2 * slot_capacity(tokens, experts) > tokens


def gate_columns(routes, groups, affinity, experts):
    weights = gate_table(routes, groups, affinity, experts)
    expert_iota = jnp.arange(experts, dtype=jnp.int32)
    hit = routes[:, :, None] == expert_iota
    return jnp.sum(jnp.where(hit, weights[:, :, None], 0.0), axis=1)


def ring_place(device, chips):
    chip = device // 2
    z, y = chip // 2, chip % 2
    return z + y * (chips - 1 - 2 * z)


def ring_chip(place, chips):
    y = place // (chips // 2)
    z = place + y * (chips - 1 - 2 * place)
    return 2 * z + y


def ring_offsets(chips):
    offsets = [0]
    for step in range(1, chips // 2 + 1):
        offsets.append(step)
        if step < chips - step:
            offsets.append(chips - step)
    return offsets


def ring_kernel(
    chips, x_ref, h_ref, gate_ref, up_hbm, down_hbm, out_ref,
    rows, part, act, from_twin, from_right, from_left, up, down,
    load_sem, send_sem, recv_sem,
):
    tokens, width = x_ref.shape
    hidden_units = down.shape[0]
    ahead, behind = chips // 2, chips - 1 - chips // 2
    offsets = ring_offsets(chips)
    blocks = {offset: block for block, offset in enumerate(offsets)}

    me = lax.axis_index("ep")
    core = me % 2
    place = ring_place(me, chips)
    right = 2 * ring_chip((place + 1) % chips, chips) + core
    left = 2 * ring_chip((place + chips - 1) % chips, chips) + core
    twin = me + 1 - 2 * core

    load_up = pltpu.make_async_copy(up_hbm.at[0, 0], up, load_sem.at[0])
    load_down = pltpu.make_async_copy(down_hbm.at[0, 0], down, load_sem.at[1])
    load_up.start()
    load_down.start()

    barrier = pltpu.get_barrier_semaphore()
    for other in (left, right, twin):
        pl.semaphore_signal(
            barrier, inc=1, device_id={"ep": other}, device_id_type=pl.DeviceIdType.MESH
        )
    pl.semaphore_wait(barrier, 3)

    copies = []

    def send(source, target, other):
        index = len(copies)
        copy = pltpu.make_async_remote_copy(
            src_ref=source,
            dst_ref=target,
            send_sem=send_sem.at[index],
            recv_sem=recv_sem.at[index],
            device_id={"ep": other},
            device_id_type=pl.DeviceIdType.MESH,
        )
        copy.start()
        copies.append(copy)
        return copy

    def mine(ref, block):
        return ref.at[pl.ds(2 * block * tokens, tokens)]

    def twins(ref, block):
        return ref.at[pl.ds((2 * block + 1) * tokens, tokens)]

    def one(ref, index):
        return ref.at[pl.ds(index * tokens, tokens)]

    def expert(block, count):
        first, size = 2 * block * tokens, 2 * count * tokens
        span = pl.ds(first, size)

        @pl.loop(0, hidden_units // 256)
        def _(tile):
            at = pl.multiple_of(tile * 256, 256)
            x = rows[span, :]
            a = jnp.dot(x, up[:, pl.ds(at, 256)], preferred_element_type=jnp.float32)
            b = jnp.dot(
                x, up[:, pl.ds(hidden_units + at, 256)], preferred_element_type=jnp.float32
            )
            act[pl.ds(0, size), pl.ds(at, 256)] = (a / (1.0 + jnp.exp(-a)) * b).astype(act.dtype)

        @pl.loop(0, width // 512)
        def _(tile):
            at = pl.multiple_of(tile * 512, 512)
            y = jnp.dot(
                act[pl.ds(0, size), :], down[:, pl.ds(at, 512)],
                preferred_element_type=jnp.float32,
            )
            part[span, pl.ds(at, 512)] = (y * gate_ref[span, :]).astype(part.dtype)

    def combine(block, *arrived):
        at = pl.ds(2 * block * tokens, tokens)
        total = part[at, :].astype(jnp.float32)
        for ref, index in ((from_twin, block),) + arrived:
            total += ref[pl.ds(index * tokens, tokens), :].astype(jnp.float32)
        return total

    def passed_on(block, *arrived):
        part[pl.ds(2 * block * tokens, tokens), :] = combine(block, *arrived).astype(part.dtype)

    gathers_right, gathers_left, forwards, swaps = {}, {}, {}, {}
    gathers_right[1] = send(x_ref, mine(rows, blocks[1]), right)
    gathers_left[1] = send(x_ref, mine(rows, blocks[chips - 1]), left)
    forwards[0] = send(x_ref, twins(rows, 0), twin)
    rows[pl.ds(0, tokens), :] = x_ref[...]
    load_up.wait()
    load_down.wait()

    def swap(block):
        swaps[block] = send(twins(part, block), one(from_twin, block), twin)

    forwards[0].wait_recv()
    expert(0, 1)
    swap(0)
    reduces_right, reduces_left = {}, {}
    for step in range(1, ahead + 1):
        group = [blocks[step]]
        gathers_right[step].wait_recv()
        if step < ahead:
            gathers_right[step + 1] = send(
                mine(rows, blocks[step]), mine(rows, blocks[step + 1]), right
            )
        forwards[blocks[step]] = send(
            mine(rows, blocks[step]), twins(rows, blocks[step]), twin
        )
        if step <= behind:
            here = blocks[chips - step]
            group.append(here)
            gathers_left[step].wait_recv()
            if step < behind:
                gathers_left[step + 1] = send(
                    mine(rows, here), mine(rows, blocks[chips - step - 1]), left
                )
            forwards[here] = send(mine(rows, here), twins(rows, here), twin)
        if step == behind + 1 and behind:
            start = blocks[chips - behind]
            swaps[start].wait_recv()
            passed_on(start)
            reduces_right[behind] = send(mine(part, start), one(from_left, behind - 1), right)
        for block in group:
            forwards[block].wait_recv()
        expert(group[0], len(group))
        for block in group:
            swap(block)

    start = blocks[ahead]
    swaps[start].wait_recv()
    passed_on(start)
    reduces_left[ahead] = send(mine(part, start), one(from_right, ahead - 1), left)
    for step in range(ahead - 1, 0, -1):
        if step < behind:
            here = blocks[chips - step]
            swaps[here].wait_recv()
            reduces_right[step + 1].wait_recv()
            passed_on(here, (from_left, step))
            reduces_right[step] = send(mine(part, here), one(from_left, step - 1), right)
        here = blocks[step]
        swaps[here].wait_recv()
        reduces_left[step + 1].wait_recv()
        passed_on(here, (from_right, step))
        reduces_left[step] = send(mine(part, here), one(from_right, step - 1), left)
    swaps[0].wait_recv()
    reduces_right[1].wait_recv()
    reduces_left[1].wait_recv()
    total = combine(0, (from_left, 0), (from_right, 0))
    out_ref[...] = (h_ref[...].astype(jnp.float32) + total).astype(out_ref.dtype)
    for copy in copies:
        copy.wait_send()


def ring_layer(hidden, gates, gain, w_gate_up, w_down):
    tokens, width = hidden.shape
    experts = lax.axis_size("ep")
    hidden_units = w_down.shape[2]
    chips = experts // 2
    ahead, behind = chips // 2, chips - 1 - chips // 2
    exchanges = 2 * (ahead + behind) + 2 * chips
    normed = rms_scale(hidden, gain)
    kind = hidden.dtype
    in_vmem = pl.BlockSpec(memory_space=pltpu.VMEM)
    in_hbm = pl.BlockSpec(memory_space=pl.ANY)
    return pl.pallas_call(
        functools.partial(ring_kernel, chips),
        out_shape=jax.ShapeDtypeStruct((tokens, width), kind),
        in_specs=[in_vmem, in_vmem, in_vmem, in_hbm, in_hbm],
        out_specs=in_vmem,
        scratch_shapes=[
            pltpu.VMEM((experts * tokens, width), kind),
            pltpu.VMEM((experts * tokens, width), kind),
            pltpu.VMEM((4 * tokens, hidden_units), kind),
            pltpu.VMEM((chips * tokens, width), kind),
            pltpu.VMEM((ahead * tokens, width), kind),
            pltpu.VMEM((behind * tokens, width), kind),
            pltpu.VMEM(w_gate_up.shape[2:], kind),
            pltpu.VMEM(w_down.shape[2:], kind),
            pltpu.SemaphoreType.DMA((2,)),
            pltpu.SemaphoreType.DMA((exchanges,)),
            pltpu.SemaphoreType.DMA((exchanges,)),
        ],
        compiler_params=pltpu.CompilerParams(
            collective_id=0, has_side_effects=True, vmem_limit_bytes=62_000_000
        ),
    )(normed, hidden, gates, w_gate_up, w_down)


def per_device(fresh, pending, expert_ids, chosen_groups, affinity, norm_gain, w_gate_up, w_down):
    at_start = lax.axis_index("pipe") == 0

    tokens, experts = pending.shape[0], lax.axis_size("ep")
    gathering = gathers_whole_blocks(tokens, experts)
    if gathering:
        columns = jnp.stack(
            [
                gate_columns(expert_ids[0, j], chosen_groups[0, j], affinity[0, j], experts)
                for j in range(2)
            ]
        )
        columns = lax.all_to_all(columns, "ep", split_axis=2, concat_axis=1, tiled=True)[:, :, 0]
        chips = experts // 2
        me = lax.axis_index("ep")
        places = (ring_place(me, chips) + chips - jnp.array(ring_offsets(chips))) % chips
        order = 2 * ring_chip(places, chips)[:, None] + jnp.stack([me % 2, 1 - me % 2])
        columns = jnp.take(columns.reshape(2, experts, tokens), order.reshape(-1), axis=1)
        columns = columns.reshape(2, experts * tokens, 1)

    def run_slot(place_index, layer_in):
        if gathering:
            return ring_layer(layer_in, columns[place_index], norm_gain[0], w_gate_up, w_down)
        return moe_layer(
            layer_in,
            expert_ids[0, place_index],
            chosen_groups[0, place_index],
            affinity[0, place_index],
            norm_gain[0],
            w_gate_up,
            w_down,
        )

    first_out = run_slot(0, jnp.where(at_start, fresh[0], pending))
    handed = from_behind(first_out, "pipe", 1)
    second_out = run_slot(1, jnp.where(at_start, fresh[1], handed))
    return jnp.stack([first_out, second_out])[None]


def solution(mesh):
    return jax.shard_map(
        per_device,
        mesh=mesh,
        in_specs=(
            P(None, "ep", None),
            P("ep", None),
            P("pipe", None, "ep", None),
            P("pipe", None, "ep", None),
            P("pipe", None, "ep", None),
            P("pipe", None),
            P("pipe", "ep", None, None),
            P("pipe", "ep", None, None),
        ),
        out_specs=P("pipe", None, "ep", None),
        check_vma=False,
    )
```

```python
import functools

import jax
import jax.numpy as jnp
from jax import lax
from jax.experimental import pallas as pl
from jax.experimental.pallas import tpu as pltpu
from jax.sharding import PartitionSpec as P

TOP = 8
GROUPS = 8


EPSILON = 1e-06
ROUTED_SCALE = 2.5


def from_behind(value, axis, steps):
    count = lax.axis_size(axis)
    first, last = (max(0, -steps), min(count, count - steps))
    return lax.ppermute(value, axis, [(source, source + steps) for source in range(first, last)])


def rms_scale(hidden, gain):
    widened = hidden.astype(jnp.float32)
    mean_square = jnp.mean(widened * widened, axis=-1, keepdims=True)
    return (widened * lax.rsqrt(mean_square + EPSILON) * gain).astype(jnp.bfloat16)


def gate_table(routes, groups, affinity, experts):
    per_group = experts // GROUPS
    owners = routes // per_group
    in_group = jnp.any(owners[:, :, None] == groups[:, None, :], axis=-1)
    summed = jnp.sum(affinity, axis=-1, keepdims=True)
    return ROUTED_SCALE * affinity * in_group.astype(jnp.float32) / summed


def slot_capacity(tokens, experts):
    spread = tokens * TOP * 5 // (4 * experts)
    needed = ((tokens - 1) * TOP + experts - TOP - 1) // (experts - TOP)
    return min(tokens, max(spread, needed))


def moe_layer(hidden, routes, groups, affinity, gain, w_gate_up, w_down):
    experts = lax.axis_size("ep")
    tokens = hidden.shape[0]
    capacity = slot_capacity(tokens, experts)
    normed = rms_scale(hidden, gain)
    weights = gate_table(routes, groups, affinity, experts)
    expert_iota = jnp.arange(experts, dtype=jnp.int32)
    matches = (routes[:, :, None] == expert_iota).astype(jnp.int32)
    per_token = jnp.sum(matches, axis=1)
    earlier = jnp.cumsum(per_token, axis=0) - per_token
    position = jnp.sum(matches * earlier[:, None, :], axis=-1)
    slot_index = routes * capacity + position
    slot_iota = jnp.arange(experts * capacity, dtype=jnp.int32)
    placing = jnp.any(slot_iota[:, None, None] == slot_index[None, :, :], axis=-1).astype(
        jnp.bfloat16
    )
    outgoing = jnp.dot(placing, normed, preferred_element_type=jnp.float32).astype(jnp.bfloat16)
    outgoing = outgoing.reshape(experts, capacity, normed.shape[1])
    hidden_units = w_down.shape[2]
    arrived_rows = lax.all_to_all(outgoing, "ep", split_axis=0, concat_axis=0, tiled=True)
    flat_rows = arrived_rows.reshape(-1, arrived_rows.shape[-1])
    joined = jnp.dot(flat_rows, w_gate_up[0, 0], preferred_element_type=jnp.float32)
    active = (jax.nn.silu(joined[:, :hidden_units]) * joined[:, hidden_units:]).astype(jnp.bfloat16)
    produced = jnp.dot(active, w_down[0, 0], preferred_element_type=jnp.float32).astype(
        jnp.bfloat16
    )
    returned = lax.all_to_all(
        produced.reshape(arrived_rows.shape), "ep", split_axis=0, concat_axis=0, tiled=True
    )
    gathered = jnp.take(returned.reshape(experts * capacity, -1), slot_index, axis=0)
    layer_out = hidden.astype(jnp.float32) + jnp.sum(
        weights[:, :, None] * gathered.astype(jnp.float32), axis=1
    )
    return layer_out.astype(jnp.bfloat16)


def gathers_whole_blocks(tokens, experts):
    ring = experts % 4 == 0 and experts > 8 and tokens % 32 == 0
    return ring and 2 * slot_capacity(tokens, experts) > tokens


def gate_columns(routes, groups, affinity, experts):
    weights = gate_table(routes, groups, affinity, experts)
    expert_iota = jnp.arange(experts, dtype=jnp.int32)
    hit = routes[:, :, None] == expert_iota
    return jnp.sum(jnp.where(hit, weights[:, :, None], 0.0), axis=1)


def ring_place(device, chips):
    chip = device // 2
    z, y = chip // 2, chip % 2
    return z + y * (chips - 1 - 2 * z)


def ring_chip(place, chips):
    y = place // (chips // 2)
    z = place + y * (chips - 1 - 2 * place)
    return 2 * z + y


def ring_offsets(chips):
    offsets = [0]
    for step in range(1, chips // 2 + 1):
        offsets.append(step)
        if step < chips - step:
            offsets.append(chips - step)
    return offsets


def ring_kernel(
    chips, first_ref, second_ref, gain_ref, gate_ref, up_hbm, down_hbm, out_ref,
    rows, part, act, from_twin, from_right, from_left, held, up, down,
    load_sem, send_sem, recv_sem, pipe_send_sem, pipe_recv_sem, done_sem,
):
    tokens, width = first_ref.shape
    half_rows = tokens // 2
    hidden_units = down.shape[0]
    ahead = chips // 2
    blocks = {offset: block for block, offset in enumerate(ring_offsets(chips))}

    me, pipe = lax.axis_index("ep"), lax.axis_index("pipe")
    core = me % 2
    place = ring_place(me, chips)
    right = 2 * ring_chip((place + 1) % chips, chips) + core
    left = 2 * ring_chip((place + chips - 1) % chips, chips) + core
    twin = me + 1 - 2 * core
    MESH = pl.DeviceIdType.MESH

    load_up = pltpu.make_async_copy(up_hbm.at[0, 0], up, load_sem.at[0])
    load_down = pltpu.make_async_copy(down_hbm.at[0, 0], down, load_sem.at[1])
    load_up.start()
    load_down.start()

    barrier = pltpu.get_barrier_semaphore()
    for other in (left, right, twin):
        pl.semaphore_signal(barrier, inc=1, device_id={"ep": other}, device_id_type=MESH)
    pl.semaphore_signal(barrier, inc=1, device_id={"pipe": 1 - pipe}, device_id_type=MESH)
    pl.semaphore_wait(barrier, 4)

    def piece(ref, start, half):
        return ref.at[pl.ds(start + half * half_rows, half_rows)]

    def mine(ref, block, half):
        return piece(ref, 2 * block * tokens, half)

    def twins(ref, block, half):
        return piece(ref, (2 * block + 1) * tokens, half)

    def behind_of(step, toward):
        return blocks[step if toward == "right" else chips - step]

    def moves(step, half, toward):
        lead = 0 if toward == "right" else 1
        return step < ahead or (step == ahead and half == lead)

    def expert_up(block, count):
        span, size = pl.ds(2 * block * tokens, 2 * count * tokens), 2 * count * tokens

        @pl.loop(0, hidden_units // 256)
        def _(tile):
            at = pl.multiple_of(tile * 256, 256)
            x = rows[span, :]
            a = jnp.dot(x, up[:, pl.ds(at, 256)], preferred_element_type=jnp.float32)
            b = jnp.dot(
                x, up[:, pl.ds(hidden_units + at, 256)], preferred_element_type=jnp.float32
            )
            act[pl.ds(0, size), pl.ds(at, 256)] = (a / (1.0 + jnp.exp(-a)) * b).astype(act.dtype)

    def expert_down(slot, block, count):
        span, size = pl.ds(2 * block * tokens, 2 * count * tokens), 2 * count * tokens

        @pl.loop(0, width // 512)
        def _(tile):
            at = pl.multiple_of(tile * 512, 512)
            y = jnp.dot(
                act[pl.ds(0, size), :], down[:, pl.ds(at, 512)],
                preferred_element_type=jnp.float32,
            )
            part[span, pl.ds(at, 512)] = (y * gate_ref[slot, span, :]).astype(part.dtype)

    def combine(block, half, *arrived):
        at = pl.ds(2 * block * tokens + half * half_rows, half_rows)
        total = part[at, :].astype(jnp.float32)
        for ref, index in ((from_twin, block),) + arrived:
            span = pl.ds(index * tokens + half * half_rows, half_rows)
            total += ref[span, :].astype(jnp.float32)
        return total

    def hand_on(half):
        return pltpu.make_async_remote_copy(
            src_ref=piece(out_ref.at[0], 0, half),
            dst_ref=piece(held, 0, half),
            send_sem=pipe_send_sem.at[half],
            recv_sem=pipe_recv_sem.at[half],
            device_id={"pipe": 1 - pipe},
            device_id_type=MESH,
        )

    for slot in range(2):
        copies = []

        def send(source, target, other):
            index = len(copies)
            copy = pltpu.make_async_remote_copy(
                src_ref=source,
                dst_ref=target,
                send_sem=send_sem.at[index],
                recv_sem=recv_sem.at[index],
                device_id={"ep": other},
                device_id_type=MESH,
            )
            copy.start()
            copies.append(copy)
            return copy

        gathers, forwards, swaps, reduces = {}, {}, {}, {}
        layer_in = held if slot else first_ref
        for half in range(2):
            at = pl.ds(half * half_rows, half_rows)
            if slot:

                @pl.when(pipe == 0)
                def _():
                    held[at, :] = second_ref[at, :]

                @pl.when(pipe == 1)
                def _():
                    hand_on(half).wait_recv()

            widened = layer_in[at, :].astype(jnp.float32)
            mean_square = jnp.mean(widened * widened, axis=-1, keepdims=True)
            normed = widened * lax.rsqrt(mean_square + EPSILON) * gain_ref[...]
            rows[at, :] = normed.astype(rows.dtype)
            source = mine(rows, 0, half)
            for toward, other in (("right", right), ("left", left)):
                target = mine(rows, behind_of(1, toward), half)
                gathers[1, half, toward] = send(source, target, other)
            forwards[0, half] = send(source, twins(rows, 0, half), twin)

        def arrive(step, half):
            for toward, other in (("right", right), ("left", left)):
                if not moves(step, half, toward):
                    continue
                here = behind_of(step, toward)
                gathers[step, half, toward].wait_recv()
                if moves(step + 1, half, toward):
                    target = mine(rows, behind_of(step + 1, toward), half)
                    gathers[step + 1, half, toward] = send(mine(rows, here, half), target, other)
                forwards[here, half] = send(
                    mine(rows, here, half), twins(rows, here, half), twin
                )

        def swap(block):
            at = pl.ds((2 * block + 1) * tokens, tokens)
            swaps[block] = send(
                part.at[at], from_twin.at[pl.ds(block * tokens, tokens)], twin
            )

        swapped = set()

        def reduce(step, half, toward):
            here = behind_of(step, "left" if toward == "right" else "right")
            if here not in swapped:
                swaps[here].wait_recv()
                swapped.add(here)
            source, other = (from_left, right) if toward == "right" else (from_right, left)
            arrived = ()
            if moves(step + 1, half, toward):
                reduces[step + 1, half, toward].wait_recv()
                arrived = ((source, step),)
            total = combine(here, half, *arrived)
            at = pl.ds(2 * here * tokens + half * half_rows, half_rows)
            part[at, :] = total.astype(part.dtype)
            target = piece(source, (step - 1) * tokens, half)
            reduces[step, half, toward] = send(mine(part, here, half), target, other)

        group = [0]
        if slot == 0:
            load_up.wait()
        for step in range(1, ahead + 1):
            for block in group:
                for half in range(2):
                    forwards[block, half].wait_recv()
            expert_up(group[0], len(group))
            arrive(step, 0)
            if step == ahead:
                arrive(step, 1)
            if slot == 0 and step == 1:
                load_down.wait()
            expert_down(slot, group[0], len(group))
            for block in group:
                swap(block)
            if step < ahead:
                arrive(step, 1)
            group = [blocks[step]] + ([blocks[chips - step]] if 2 * step < chips else [])
        reduce(ahead - 1, 1, "right")
        reduce(ahead - 1, 0, "left")
        for half in range(2):
            forwards[group[0], half].wait_recv()
        expert_up(group[0], 1)
        expert_down(slot, group[0], 1)
        swap(group[0])
        for step in range(ahead, 0, -1):
            reduce(step, 0, "right")
            reduce(step, 1, "left")
            if step > 2:
                reduce(step - 2, 1, "right")
                reduce(step - 2, 0, "left")
        swaps[0].wait_recv()
        for half in range(2):
            reduces[1, half, "right"].wait_recv()
            reduces[1, half, "left"].wait_recv()
            at = pl.ds(half * half_rows, half_rows)
            total = combine(0, half, (from_left, 0), (from_right, 0))
            result = layer_in[at, :].astype(jnp.float32) + total
            out_ref[slot, at, :] = result.astype(out_ref.dtype)
            if slot == 0:

                @pl.when(pipe == 0)
                def _():
                    hand_on(half).start()

        for copy in copies:
            copy.wait_send()
        if slot == 0:
            for other in (left, right, twin):
                pl.semaphore_signal(done_sem, inc=1, device_id={"ep": other}, device_id_type=MESH)
            pl.semaphore_wait(done_sem, 3)

    @pl.when(pipe == 0)
    def _():
        hand_on(0).wait_send()
        hand_on(1).wait_send()


def ring_relay(first, second, gates, gain, w_gate_up, w_down):
    tokens, width = first.shape
    experts = lax.axis_size("ep")
    hidden_units = w_down.shape[2]
    chips = experts // 2
    exchanges = 4 * (chips - 1) + 3 * chips
    kind = first.dtype
    in_vmem = pl.BlockSpec(memory_space=pltpu.VMEM)
    in_hbm = pl.BlockSpec(memory_space=pl.ANY)
    return pl.pallas_call(
        functools.partial(ring_kernel, chips),
        out_shape=jax.ShapeDtypeStruct((2, tokens, width), kind),
        in_specs=[in_vmem] * 4 + [in_hbm] * 2,
        out_specs=in_vmem,
        scratch_shapes=[
            pltpu.VMEM((experts * tokens, width), kind),
            pltpu.VMEM((experts * tokens, width), kind),
            pltpu.VMEM((4 * tokens, hidden_units), kind),
            pltpu.VMEM((chips * tokens, width), kind),
            pltpu.VMEM((chips // 2 * tokens, width), kind),
            pltpu.VMEM((chips // 2 * tokens, width), kind),
            pltpu.VMEM((tokens, width), kind),
            pltpu.VMEM(w_gate_up.shape[2:], kind),
            pltpu.VMEM(w_down.shape[2:], kind),
            pltpu.SemaphoreType.DMA((2,)),
            pltpu.SemaphoreType.DMA((exchanges,)),
            pltpu.SemaphoreType.DMA((exchanges,)),
            pltpu.SemaphoreType.DMA((2,)),
            pltpu.SemaphoreType.DMA((2,)),
            pltpu.SemaphoreType.REGULAR,
        ],
        compiler_params=pltpu.CompilerParams(
            collective_id=0, has_side_effects=True, vmem_limit_bytes=62_000_000
        ),
    )(first, second, gain, gates, w_gate_up, w_down)


def per_device(fresh, pending, expert_ids, chosen_groups, affinity, norm_gain, w_gate_up, w_down):
    at_start = lax.axis_index("pipe") == 0

    tokens, experts = pending.shape[0], lax.axis_size("ep")
    if lax.axis_size("pipe") == 2 and gathers_whole_blocks(tokens, experts):
        columns = jnp.stack(
            [
                gate_columns(expert_ids[0, j], chosen_groups[0, j], affinity[0, j], experts)
                for j in range(2)
            ]
        )
        columns = lax.all_to_all(columns, "ep", split_axis=2, concat_axis=1, tiled=True)[:, :, 0]
        chips = experts // 2
        me = lax.axis_index("ep")
        places = (ring_place(me, chips) + chips - jnp.array(ring_offsets(chips))) % chips
        order = 2 * ring_chip(places, chips)[:, None] + jnp.stack([me % 2, 1 - me % 2])
        columns = jnp.take(columns.reshape(2, experts, tokens), order.reshape(-1), axis=1)
        columns = columns.reshape(2, experts * tokens, 1)
        first = jnp.where(at_start, fresh[0], pending)
        return ring_relay(first, fresh[1], columns, norm_gain, w_gate_up, w_down)[None, :]

    def run_slot(place_index, layer_in):
        return moe_layer(
            layer_in,
            expert_ids[0, place_index],
            chosen_groups[0, place_index],
            affinity[0, place_index],
            norm_gain[0],
            w_gate_up,
            w_down,
        )

    first_out = run_slot(0, jnp.where(at_start, fresh[0], pending))
    handed = from_behind(first_out, "pipe", 1)
    second_out = run_slot(1, jnp.where(at_start, fresh[1], handed))
    return jnp.stack([first_out, second_out])[None]


def solution(mesh):
    return jax.shard_map(
        per_device,
        mesh=mesh,
        in_specs=(
            P(None, "ep", None),
            P("ep", None),
            P("pipe", None, "ep", None),
            P("pipe", None, "ep", None),
            P("pipe", None, "ep", None),
            P("pipe", None),
            P("pipe", "ep", None, None),
            P("pipe", "ep", None, None),
        ),
        out_specs=P("pipe", None, "ep", None),
        check_vma=False,
    )
```

```python
import functools

import jax
import jax.numpy as jnp
from jax import lax
from jax.experimental import pallas as pl
from jax.experimental.pallas import tpu as pltpu
from jax.sharding import PartitionSpec as P

TOP = 8
GROUPS = 8
LANES = 128


EPSILON = 1e-06
ROUTED_SCALE = 2.5


def from_behind(value, axis, steps):
    count = lax.axis_size(axis)
    first, last = (max(0, -steps), min(count, count - steps))
    return lax.ppermute(value, axis, [(source, source + steps) for source in range(first, last)])


def rms_scale(hidden, gain):
    widened = hidden.astype(jnp.float32)
    mean_square = jnp.mean(widened * widened, axis=-1, keepdims=True)
    return (widened * lax.rsqrt(mean_square + EPSILON) * gain).astype(jnp.bfloat16)


def gate_table(routes, groups, affinity, experts):
    per_group = experts // GROUPS
    owners = routes // per_group
    in_group = jnp.any(owners[:, :, None] == groups[:, None, :], axis=-1)
    summed = jnp.sum(affinity, axis=-1, keepdims=True)
    return ROUTED_SCALE * affinity * in_group.astype(jnp.float32) / summed


def slot_capacity(tokens, experts):
    spread = tokens * TOP * 5 // (4 * experts)
    needed = ((tokens - 1) * TOP + experts - TOP - 1) // (experts - TOP)
    return min(tokens, max(spread, needed))


def moe_layer(hidden, routes, groups, affinity, gain, w_gate_up, w_down):
    experts = lax.axis_size("ep")
    tokens = hidden.shape[0]
    capacity = slot_capacity(tokens, experts)
    normed = rms_scale(hidden, gain)
    weights = gate_table(routes, groups, affinity, experts)
    expert_iota = jnp.arange(experts, dtype=jnp.int32)
    matches = (routes[:, :, None] == expert_iota).astype(jnp.int32)
    per_token = jnp.sum(matches, axis=1)
    earlier = jnp.cumsum(per_token, axis=0) - per_token
    position = jnp.sum(matches * earlier[:, None, :], axis=-1)
    slot_index = routes * capacity + position
    slot_iota = jnp.arange(experts * capacity, dtype=jnp.int32)
    placing = jnp.any(slot_iota[:, None, None] == slot_index[None, :, :], axis=-1).astype(
        jnp.bfloat16
    )
    outgoing = jnp.dot(placing, normed, preferred_element_type=jnp.float32).astype(jnp.bfloat16)
    outgoing = outgoing.reshape(experts, capacity, normed.shape[1])
    hidden_units = w_down.shape[2]
    arrived_rows = lax.all_to_all(outgoing, "ep", split_axis=0, concat_axis=0, tiled=True)
    flat_rows = arrived_rows.reshape(-1, arrived_rows.shape[-1])
    joined = jnp.dot(flat_rows, w_gate_up[0, 0], preferred_element_type=jnp.float32)
    active = (jax.nn.silu(joined[:, :hidden_units]) * joined[:, hidden_units:]).astype(jnp.bfloat16)
    produced = jnp.dot(active, w_down[0, 0], preferred_element_type=jnp.float32).astype(
        jnp.bfloat16
    )
    returned = lax.all_to_all(
        produced.reshape(arrived_rows.shape), "ep", split_axis=0, concat_axis=0, tiled=True
    )
    gathered = jnp.take(returned.reshape(experts * capacity, -1), slot_index, axis=0)
    layer_out = hidden.astype(jnp.float32) + jnp.sum(
        weights[:, :, None] * gathered.astype(jnp.float32), axis=1
    )
    return layer_out.astype(jnp.bfloat16)


def gathers_whole_blocks(tokens, experts):
    ring = experts % 4 == 0 and experts > 8 and tokens % 32 == 0 and 2 * experts <= LANES
    return ring and 2 * slot_capacity(tokens, experts) > tokens


def gate_columns(routes, groups, affinity, experts):
    weights = gate_table(routes, groups, affinity, experts)
    expert_iota = jnp.arange(LANES, dtype=jnp.int32) % experts
    hit = routes[:, :, None] == expert_iota
    return jnp.sum(jnp.where(hit, weights[:, :, None], 0.0), axis=1)


def ring_place(device, chips):
    chip = device // 2
    z, y = chip // 2, chip % 2
    return z + y * (chips - 1 - 2 * z)


def ring_chip(place, chips):
    y = place // (chips // 2)
    z = place + y * (chips - 1 - 2 * place)
    return 2 * z + y


def ring_offsets(chips):
    offsets = [0]
    for step in range(1, chips // 2 + 1):
        offsets.append(step)
        if step < chips - step:
            offsets.append(chips - step)
    return offsets


def ring_kernel(
    chips, fresh_ref, pending_ref, gain_ref, gate_ref, up_hbm, down_hbm, out_ref,
    rows, part, act, from_twin, from_right, from_left, held, up, down,
    load_sem, send_sem, recv_sem, pipe_send_sem, pipe_recv_sem, done_sem,
):
    tokens, width = pending_ref.shape
    half_rows = tokens // 2
    experts, lanes = 2 * chips, gate_ref.shape[2]
    hidden_units = down.shape[0]
    ahead = chips // 2
    blocks = {offset: block for block, offset in enumerate(ring_offsets(chips))}

    me, pipe = lax.axis_index("ep"), lax.axis_index("pipe")
    core = me % 2
    place = ring_place(me, chips)
    right = 2 * ring_chip((place + 1) % chips, chips) + core
    left = 2 * ring_chip((place + chips - 1) % chips, chips) + core
    twin = me + 1 - 2 * core
    MESH = pl.DeviceIdType.MESH

    load_up = pltpu.make_async_copy(up_hbm.at[0, 0], up, load_sem.at[0])
    load_down = pltpu.make_async_copy(down_hbm.at[0, 0], down, load_sem.at[1])
    load_up.start()
    load_down.start()

    barrier = pltpu.get_barrier_semaphore()
    for other in (left, right, twin):
        pl.semaphore_signal(barrier, inc=1, device_id={"ep": other}, device_id_type=MESH)
    pl.semaphore_signal(barrier, inc=1, device_id={"pipe": 1 - pipe}, device_id_type=MESH)
    pl.semaphore_wait(barrier, 4)

    def piece(ref, start, half):
        return ref.at[pl.ds(start + half * half_rows, half_rows)]

    def mine(ref, block, half):
        return piece(ref, 2 * block * tokens, half)

    def twins(ref, block, half):
        return piece(ref, (2 * block + 1) * tokens, half)

    def behind_of(step, toward):
        return blocks[step if toward == "right" else chips - step]

    def moves(step, half, toward):
        lead = 0 if toward == "right" else 1
        return step < ahead or (step == ahead and half == lead)

    def expert_up(block, count):
        span, size = pl.ds(2 * block * tokens, 2 * count * tokens), 2 * count * tokens

        @pl.loop(0, hidden_units // 256)
        def _(tile):
            at = pl.multiple_of(tile * 256, 256)
            x = rows[span, pl.ds(0, width)]
            a = jnp.dot(x, up[:, pl.ds(at, 256)], preferred_element_type=jnp.float32)
            b = jnp.dot(
                x, up[:, pl.ds(hidden_units + at, 256)], preferred_element_type=jnp.float32
            )
            act[pl.ds(0, size), pl.ds(at, 256)] = (a / (1.0 + jnp.exp(-a)) * b).astype(act.dtype)

    def expert_down(block, count):
        span, size = pl.ds(2 * block * tokens, 2 * count * tokens), 2 * count * tokens
        lane = lax.broadcasted_iota(jnp.int32, (size, lanes), 1)
        parts = rows[span, pl.ds(width, lanes)].astype(jnp.float32)
        ours = (lane == me) | (lane == experts + me)
        gate = jnp.sum(jnp.where(ours, parts, 0.0), axis=1, keepdims=True)

        @pl.loop(0, width // 512)
        def _(tile):
            at = pl.multiple_of(tile * 512, 512)
            y = jnp.dot(
                act[pl.ds(0, size), :], down[:, pl.ds(at, 512)],
                preferred_element_type=jnp.float32,
            )
            part[span, pl.ds(at, 512)] = (y * gate).astype(part.dtype)

    def combine(block, half, *arrived):
        at = pl.ds(2 * block * tokens + half * half_rows, half_rows)
        total = part[at, :].astype(jnp.float32)
        for ref, index in ((from_twin, block),) + arrived:
            span = pl.ds(index * tokens + half * half_rows, half_rows)
            total += ref[span, :].astype(jnp.float32)
        return total

    def hand_on(half):
        return pltpu.make_async_remote_copy(
            src_ref=piece(out_ref.at[0], 0, half),
            dst_ref=piece(held, 0, half),
            send_sem=pipe_send_sem.at[half],
            recv_sem=pipe_recv_sem.at[half],
            device_id={"pipe": 1 - pipe},
            device_id_type=MESH,
        )

    def layer_in(slot, at):
        if slot:
            return held[at, :].astype(jnp.float32)
        fresh, pending = fresh_ref[0, at, :], pending_ref[at, :]
        return jnp.where(pipe == 0, fresh.astype(jnp.float32), pending.astype(jnp.float32))

    for slot in range(2):
        copies = []

        def send(source, target, other):
            index = len(copies)
            copy = pltpu.make_async_remote_copy(
                src_ref=source,
                dst_ref=target,
                send_sem=send_sem.at[index],
                recv_sem=recv_sem.at[index],
                device_id={"ep": other},
                device_id_type=MESH,
            )
            copy.start()
            copies.append(copy)
            return copy

        gathers, forwards, swaps, reduces = {}, {}, {}, {}
        for half in range(2):
            at = pl.ds(half * half_rows, half_rows)
            if slot:

                @pl.when(pipe == 0)
                def _():
                    held[at, :] = fresh_ref[1, at, :]

                @pl.when(pipe == 1)
                def _():
                    hand_on(half).wait_recv()

            widened = layer_in(slot, at)
            mean_square = jnp.mean(widened * widened, axis=-1, keepdims=True)
            normed = widened * lax.rsqrt(mean_square + EPSILON) * gain_ref[...]
            rows[at, pl.ds(0, width)] = normed.astype(rows.dtype)
            gate = gate_ref[slot, at, :]
            high = gate.astype(rows.dtype).astype(jnp.float32)
            lane = lax.broadcasted_iota(jnp.int32, gate.shape, 1)
            packed = jnp.where(lane < experts, high, gate - high)
            rows[at, pl.ds(width, lanes)] = packed.astype(rows.dtype)
            source = mine(rows, 0, half)
            for toward, other in (("right", right), ("left", left)):
                target = mine(rows, behind_of(1, toward), half)
                gathers[1, half, toward] = send(source, target, other)
            forwards[0, half] = send(source, twins(rows, 0, half), twin)

        def arrive(step, half):
            for toward, other in (("right", right), ("left", left)):
                if not moves(step, half, toward):
                    continue
                here = behind_of(step, toward)
                gathers[step, half, toward].wait_recv()
                if moves(step + 1, half, toward):
                    target = mine(rows, behind_of(step + 1, toward), half)
                    gathers[step + 1, half, toward] = send(mine(rows, here, half), target, other)
                forwards[here, half] = send(
                    mine(rows, here, half), twins(rows, here, half), twin
                )

        def swap(block):
            at = pl.ds((2 * block + 1) * tokens, tokens)
            swaps[block] = send(
                part.at[at], from_twin.at[pl.ds(block * tokens, tokens)], twin
            )

        swapped = set()

        def reduce(step, half, toward):
            here = behind_of(step, "left" if toward == "right" else "right")
            if here not in swapped:
                swaps[here].wait_recv()
                swapped.add(here)
            source, other = (from_left, right) if toward == "right" else (from_right, left)
            arrived = ()
            if moves(step + 1, half, toward):
                reduces[step + 1, half, toward].wait_recv()
                arrived = ((source, step),)
            total = combine(here, half, *arrived)
            at = pl.ds(2 * here * tokens + half * half_rows, half_rows)
            part[at, :] = total.astype(part.dtype)
            target = piece(source, (step - 1) * tokens, half)
            reduces[step, half, toward] = send(mine(part, here, half), target, other)

        group = [0]
        if slot == 0:
            load_up.wait()
        for step in range(1, ahead + 1):
            for block in group:
                for half in range(2):
                    forwards[block, half].wait_recv()
            expert_up(group[0], len(group))
            arrive(step, 0)
            if step == ahead:
                arrive(step, 1)
            if slot == 0 and step == 1:
                load_down.wait()
            expert_down(group[0], len(group))
            for block in group:
                swap(block)
            if step < ahead:
                arrive(step, 1)
            group = [blocks[step]] + ([blocks[chips - step]] if 2 * step < chips else [])
        reduce(ahead - 1, 1, "right")
        reduce(ahead - 1, 0, "left")
        for half in range(2):
            forwards[group[0], half].wait_recv()
        expert_up(group[0], 1)
        expert_down(group[0], 1)
        swap(group[0])
        for step in range(ahead, 0, -1):
            reduce(step, 0, "right")
            reduce(step, 1, "left")
            if step > 2:
                reduce(step - 2, 1, "right")
                reduce(step - 2, 0, "left")
        swaps[0].wait_recv()
        for half in range(2):
            reduces[1, half, "right"].wait_recv()
            reduces[1, half, "left"].wait_recv()
            at = pl.ds(half * half_rows, half_rows)
            total = combine(0, half, (from_left, 0), (from_right, 0))
            result = layer_in(slot, at) + total
            out_ref[slot, at, :] = result.astype(out_ref.dtype)
            if slot == 0:

                @pl.when(pipe == 0)
                def _():
                    hand_on(half).start()

        for copy in copies:
            copy.wait_send()
        if slot == 0:
            for other in (left, right, twin):
                pl.semaphore_signal(done_sem, inc=1, device_id={"ep": other}, device_id_type=MESH)
            pl.semaphore_wait(done_sem, 3)

    @pl.when(pipe == 0)
    def _():
        hand_on(0).wait_send()
        hand_on(1).wait_send()


def ring_relay(fresh, pending, gates, gain, w_gate_up, w_down):
    tokens, width = pending.shape
    experts = lax.axis_size("ep")
    hidden_units = w_down.shape[2]
    chips = experts // 2
    exchanges = 4 * (chips - 1) + 3 * chips
    kind = pending.dtype
    in_vmem = pl.BlockSpec(memory_space=pltpu.VMEM)
    in_hbm = pl.BlockSpec(memory_space=pl.ANY)
    return pl.pallas_call(
        functools.partial(ring_kernel, chips),
        out_shape=jax.ShapeDtypeStruct((2, tokens, width), kind),
        in_specs=[in_vmem] * 4 + [in_hbm] * 2,
        out_specs=in_vmem,
        scratch_shapes=[
            pltpu.VMEM((experts * tokens, width + gates.shape[2]), kind),
            pltpu.VMEM((experts * tokens, width), kind),
            pltpu.VMEM((4 * tokens, hidden_units), kind),
            pltpu.VMEM((chips * tokens, width), kind),
            pltpu.VMEM((chips // 2 * tokens, width), kind),
            pltpu.VMEM((chips // 2 * tokens, width), kind),
            pltpu.VMEM((tokens, width), kind),
            pltpu.VMEM(w_gate_up.shape[2:], kind),
            pltpu.VMEM(w_down.shape[2:], kind),
            pltpu.SemaphoreType.DMA((2,)),
            pltpu.SemaphoreType.DMA((exchanges,)),
            pltpu.SemaphoreType.DMA((exchanges,)),
            pltpu.SemaphoreType.DMA((2,)),
            pltpu.SemaphoreType.DMA((2,)),
            pltpu.SemaphoreType.REGULAR,
        ],
        compiler_params=pltpu.CompilerParams(
            collective_id=0, has_side_effects=True, vmem_limit_bytes=62_000_000
        ),
    )(fresh, pending, gain, gates, w_gate_up, w_down)


def per_device(fresh, pending, expert_ids, chosen_groups, affinity, norm_gain, w_gate_up, w_down):
    at_start = lax.axis_index("pipe") == 0

    tokens, experts = pending.shape[0], lax.axis_size("ep")
    if lax.axis_size("pipe") == 2 and gathers_whole_blocks(tokens, experts):
        columns = jnp.stack(
            [
                gate_columns(expert_ids[0, j], chosen_groups[0, j], affinity[0, j], experts)
                for j in range(2)
            ]
        )
        return ring_relay(fresh, pending, columns, norm_gain, w_gate_up, w_down)[None, :]

    def run_slot(place_index, layer_in):
        return moe_layer(
            layer_in,
            expert_ids[0, place_index],
            chosen_groups[0, place_index],
            affinity[0, place_index],
            norm_gain[0],
            w_gate_up,
            w_down,
        )

    first_out = run_slot(0, jnp.where(at_start, fresh[0], pending))
    handed = from_behind(first_out, "pipe", 1)
    second_out = run_slot(1, jnp.where(at_start, fresh[1], handed))
    return jnp.stack([first_out, second_out])[None]


def solution(mesh):
    return jax.shard_map(
        per_device,
        mesh=mesh,
        in_specs=(
            P(None, "ep", None),
            P("ep", None),
            P("pipe", None, "ep", None),
            P("pipe", None, "ep", None),
            P("pipe", None, "ep", None),
            P("pipe", None),
            P("pipe", "ep", None, None),
            P("pipe", "ep", None, None),
        ),
        out_specs=P("pipe", None, "ep", None),
        check_vma=False,
    )
```
